512 devices in a mesh: db: 64 (over y, z), heads: 8 (over x, core).
Axes of the slice: x: 4, y: 8, z: 8, core: 2. Of those that a mesh axis runs over, the one named last changes fastest.
Arguments:
- queries: bfloat16 [32768, 3072], P('db', 'heads'), may hold values from -80 to 80
- neighbour_ids: int32 [512, 2], P('db'), may hold values from 0 to 383, as said below
- cache_keys: bfloat16 [384, 128, 1024], P('db', None, 'heads'), may hold values from -16 to 16
- cache_values: bfloat16 [384, 128, 1024], P('db', None, 'heads'), may hold values from -6 to 6
- out_grad: bfloat16 [32768, 3072], P('db', 'heads'), may hold values from -6 to 6
Outputs:
- query_grad: bfloat16 [32768, 3072], P('db', 'heads')
The draws below stay inside these ranges and needn't reach their ends.
Inputs may be any that keep to these rules, and one draw needn't show every extreme that they name: `neighbour_ids`: entry e is held by index floor(e / 6) of db. Among the 16 neighbours of the spans of one index of db (aligned blocks of 8 rows), at most 2 are held by any one index of db, and one index of db, the same for every block, holds exactly 2 of them in every block. Every other index of db holds at most one neighbour of a block.
All inputs are finite; a program needn't handle non-finite values.
Results may differ from the reference program's by a relative error of at most 0.014.
Values may be sent and summed in bfloat16 or wider, within the bound.
No kernel may reach another device: no remote copies, remote signals or barrier semaphores. Data moves between devices by JAX's collectives and lax.ppermute only.
A program may use at most 64 MiB of HBM per device.

```python
import math
import jax
import jax.numpy as jnp
from jax import lax

HD = 128
KVH = 8
GROUP = 3
SPAN = 64
ENT_LEN = 128
TOK_DEV = 512
ENT_DEV = 6
QH = 24
CH_DEV = 8
TOKENS = 32768
SPANS = 512
LENGTH = 4096
ENTRIES = 384
MOST = 2


def neighbour_table(key):
    base_key = jax.random.fold_in(key, 101)
    holders_all = SPANS // CH_DEV
    wanted_count = 2 * CH_DEV
    hot_key, perm_key, order_key, entry_key = jax.random.split(base_key, 4)
    hottest = jax.random.randint(hot_key, (), 0, holders_all)
    perm_keys = jax.random.split(perm_key, holders_all * MOST)
    shuffles = jax.vmap(lambda subkey: jax.random.permutation(subkey, holders_all - 1))(perm_keys)
    others = shuffles.reshape(holders_all, MOST * (holders_all - 1))[:, :wanted_count - MOST].astype(jnp.int32)
    others = others + (others >= hottest).astype(jnp.int32)
    hot_part = jnp.zeros((holders_all, MOST), jnp.int32) + hottest
    owners = jnp.concatenate([hot_part, others], axis=1)
    order_keys = jax.random.split(order_key, holders_all)
    orders = jax.vmap(lambda subkey: jax.random.permutation(subkey, wanted_count))(order_keys)
    owners = jnp.take_along_axis(owners, orders.astype(jnp.int32), axis=1)
    entry_draws = jax.random.randint(entry_key, (3, holders_all, wanted_count), 0, ENT_DEV)
    local_entry = jnp.min(entry_draws, axis=0)
    return (owners * ENT_DEV + local_entry).reshape(SPANS, 2).astype(jnp.int32)


def key_table(key):
    base_key = jax.random.fold_in(key, 202)
    values_raw = jnp.clip(jax.random.normal(base_key, (ENTRIES, ENT_LEN, KVH * HD), jnp.float32), -4.0, 4.0)
    return values_raw


def draw_neighbour_ids(key, part):
    return neighbour_table(key)


def draw_cache_keys(key, part):
    return key_table(key).astype(jnp.bfloat16)


def draw_queries(key, part):
    base_key = jax.random.fold_in(key, 303)
    row_width = KVH * GROUP * HD
    noise = jnp.clip(jax.random.normal(base_key, (TOKENS, row_width), jnp.float32), -6.0, 6.0)
    return noise.astype(jnp.bfloat16)


def levels(key, shape, pieces, least, top_value):
    loudness = 1.0
    for axis_at, shards_of in pieces:
        draws = jax.random.uniform(jax.random.fold_in(jax.random.fold_in(key, 6), axis_at), (shards_of,), jnp.float32, least / len(pieces), top_value / len(pieces))
        loudness = loudness * jnp.repeat(jnp.exp(draws), shape[axis_at] // shards_of).reshape((-1,) + (1,) * (len(shape) - 1 - axis_at))
    return loudness


def scatter_about(own_key, extent, deviation, bound, pieces=(), kind=jnp.bfloat16):
    level = levels(own_key, extent, pieces, -0.22, 0.18) if pieces else 1.0
    entries = jax.random.normal(own_key, extent, jnp.float32) * deviation * level
    return jnp.minimum(jnp.maximum(entries, -bound), bound).astype(kind)


def setup_inputs(seed: int = 0) -> dict:
    seeds = jax.random.split(jax.random.key(seed), 6)
    queries = draw_queries(jax.random.fold_in(seeds[5], 71), 0)
    neighbour_ids = draw_neighbour_ids(jax.random.fold_in(seeds[5], 71), 0)
    cache_keys = draw_cache_keys(jax.random.fold_in(seeds[5], 71), 0)
    cache_values = scatter_about(seeds[3], (ENTRIES, ENT_LEN, KVH * HD), 1.0, 6.0, ((0, 64), (2, 8)))
    out_grad = scatter_about(seeds[4], (TOKENS, QH * HD), 1.0, 6.0, ((0, 64), (1, 8)))
    return {"queries": queries, "neighbour_ids": neighbour_ids, "cache_keys": cache_keys, "cache_values": cache_values, "out_grad": out_grad}


def attend(query_block, grad_block, key_rows, value_rows, valid_rows):
    factor = 1.0 / math.sqrt(HD)
    query_wide = query_block.astype(jnp.float32)
    grad_wide = grad_block.astype(jnp.float32)
    key_wide = key_rows.astype(jnp.float32)
    value_wide = value_rows.astype(jnp.float32)
    scores = jnp.einsum('ihgd,khd->hgik', query_wide, key_wide) * factor
    highest = lax.optimization_barrier(jnp.max(scores, axis=-1, keepdims=True))
    expo = jnp.exp(scores - highest)
    probs = expo / lax.optimization_barrier(jnp.sum(expo, axis=-1, keepdims=True))
    probs = jnp.where(valid_rows[None, None, :, None], probs, 0.0)
    probs_low = lax.optimization_barrier(probs.astype(jnp.bfloat16)).astype(jnp.float32)
    attended = jnp.einsum('hgik,khd->ihgd', probs_low, value_wide)
    attended = lax.optimization_barrier(attended.astype(jnp.bfloat16)).astype(jnp.float32)
    along = jnp.einsum('ihgd,khd->hgik', grad_wide, value_wide)
    delta = jnp.einsum('ihgd,ihgd->hgi', grad_wide, attended)
    slope = probs * (along - delta[..., None])
    slope = lax.optimization_barrier(slope.astype(jnp.bfloat16)).astype(jnp.float32)
    result = jnp.einsum('hgik,khd->ihgd', slope, key_wide) * factor
    return result.astype(jnp.bfloat16)

def reference(queries, neighbour_ids, cache_keys, cache_values, out_grad):
    row_width = KVH * GROUP * HD
    front_pad = jnp.zeros((1, row_width), jnp.bfloat16)
    back_pad = jnp.zeros((SPAN - 1, row_width), jnp.bfloat16)
    query_ext = jnp.concatenate([front_pad, queries, back_pad], axis=0).reshape(SPANS + 1, SPAN, KVH, GROUP, HD)
    grad_ext = jnp.concatenate([front_pad, out_grad, back_pad], axis=0).reshape(SPANS + 1, SPAN, KVH, GROUP, HD)
    list_ext = jnp.concatenate([neighbour_ids[:1], neighbour_ids], axis=0).astype(jnp.int32)
    token_index = jnp.arange((SPANS + 1) * SPAN, dtype=jnp.int32).reshape(SPANS + 1, SPAN) - 1
    valid_ext = (token_index >= SPAN - 1) & (token_index < TOKENS) & ((token_index + TOK_DEV // 2) % LENGTH >= SPAN - 1)

    def one_block(operands):
        query_block, grad_block, entry_pair, valid_rows = operands
        key_rows = jnp.take(cache_keys, entry_pair, axis=0).reshape(2 * ENT_LEN, KVH, HD)
        value_rows = jnp.take(cache_values, entry_pair, axis=0).reshape(2 * ENT_LEN, KVH, HD)
        return attend(query_block, grad_block, key_rows, value_rows, valid_rows)
    grads = lax.map(one_block, (query_ext, grad_ext, list_ext, valid_ext))
    return grads.reshape((SPANS + 1) * SPAN, row_width)[1:TOKENS + 1]
```

```python
import math

import jax
import jax.numpy as jnp
from jax import lax
from jax.experimental import pallas as pl
from jax.experimental.pallas import tpu as pltpu
from jax.sharding import PartitionSpec as P

HD = 128
GROUP = 3
SPAN = 64
LENGTH = 4096
TAIL = 16


def pack_kernel(ids_ref, keys_ref, values_ref, out_ref):
    entries, pieces = keys_ref.shape[:2]
    holders, chunks, piece, channels = out_ref.shape
    spans = ids_ref.shape[0]
    lane = lax.broadcasted_iota(jnp.int32, (piece, channels), 1)
    places = jnp.zeros((piece, channels), jnp.int32)
    for c in range(2 * spans):
        wanted_id = ids_ref[c // 2, c % 2]
        place = (wanted_id // entries) * chunks + wanted_id % entries - holders * chunks // 2
        places = jnp.where(lane == c, place, places)
    places = places.astype(jnp.float32).astype(jnp.bfloat16)
    for e in range(entries):
        out_ref[0:pieces, e] = keys_ref[e]
        out_ref[pieces : 2 * pieces, e] = values_ref[e]
    out_ref[:, entries] = jnp.broadcast_to(places[None], (holders, piece, channels))


def pick_kernel(index_ref, table_ref, out_ref):
    dests, slots = out_ref.shape[:2]
    wanted = slots - 2

    def one_dest(d, carry):
        for c in range(slots):
            out_ref[d, c] = table_ref[index_ref[d * wanted + c]]
        return carry

    lax.fori_loop(0, dests, one_dest, 0)


def attend(query_rows, grad_rows, keys, values):
    factor = 1.0 / math.sqrt(HD)
    contract = (((1,), (1,)), ((), ()))
    scores = (
        lax.dot_general(query_rows, keys, contract, preferred_element_type=jnp.float32) * factor
    )
    along = lax.dot_general(grad_rows, values, contract, preferred_element_type=jnp.float32)
    expo = jnp.exp(scores - jnp.max(scores, axis=-1, keepdims=True))
    probs = expo / jnp.sum(expo, axis=-1, keepdims=True)
    delta = jnp.sum(probs * along, axis=-1, keepdims=True)
    slope = (probs * (along - delta)).astype(jnp.bfloat16)
    return jnp.dot(slope, keys, preferred_element_type=jnp.float32) * factor


def attend_kernel(start_ref, query_ref, grad_ref, rows_ref, out_ref):
    tokens = query_ref.shape[0]
    blocks = tokens // SPAN
    pieces = rows_ref.shape[0] // 2
    half_shift = tokens // 2
    start = start_ref[0]

    def stacked(ref, parts):
        return jnp.concatenate(
            [ref[a:b, g * HD : (g + 1) * HD] for g in range(GROUP) for a, b in parts], axis=0
        )

    held = None
    for k in range(-1, blocks):
        keys = rows_ref[0:pieces, k + 1].reshape(pieces * 8, HD)
        values = rows_ref[pieces : 2 * pieces, k + 1].reshape(pieces * 8, HD)
        parts = []
        if k >= 0:
            parts.append(((k + 1) * SPAN - TAIL, (k + 1) * SPAN))
        if k + 1 < blocks:
            parts.append(((k + 1) * SPAN, (k + 2) * SPAN))
        result = attend(stacked(query_ref, parts), stacked(grad_ref, parts), keys, values)
        height = sum(b - a for a, b in parts)
        by_head = [result[g * height : (g + 1) * height] for g in range(GROUP)]
        if k >= 0:
            last = lax.broadcasted_iota(jnp.int32, (SPAN, HD), 0) == SPAN - 1
            token = start + k * SPAN + lax.broadcasted_iota(jnp.int32, (SPAN, HD), 0)
            valid = (token >= SPAN - 1) & ((token + half_shift) % LENGTH >= SPAN - 1)
            for g in range(GROUP):
                tail = by_head[g][:TAIL]
                here = jnp.concatenate([held[g][: SPAN - TAIL], jnp.where(last[SPAN - TAIL :], tail, held[g][SPAN - TAIL :])], axis=0)
                out_ref[k * SPAN : (k + 1) * SPAN, g * HD : (g + 1) * HD] = jnp.where(
                    valid, here, 0.0
                ).astype(out_ref.dtype)
        held = [r[TAIL if k >= 0 else 0 :] for r in by_head]


def body(queries, neighbour_ids, cache_keys, cache_values, out_grad):
    holders = lax.axis_size("db")
    me = lax.axis_index("db")
    entries, entry_rows, channels = cache_keys.shape
    tokens, width = queries.shape
    spans = neighbour_ids.shape[0]
    wanted = 2 * spans
    pieces = holders // 2
    piece = entry_rows // pieces
    chunks = entries + 1
    middle = holders * chunks // 2
    vmem = pl.BlockSpec(memory_space=pltpu.VMEM)
    smem = pl.BlockSpec(memory_space=pltpu.SMEM)
    small = pltpu.CompilerParams(vmem_limit_bytes=16 * 2**20)

    packed = pl.pallas_call(
        pack_kernel,
        out_shape=jax.ShapeDtypeStruct((holders, chunks, piece, channels), jnp.bfloat16),
        in_specs=[smem, vmem, vmem],
        out_specs=vmem,
        compiler_params=small,
    )(
        neighbour_ids,
        cache_keys.reshape(entries, pieces, piece, channels),
        cache_values.reshape(entries, pieces, piece, channels),
    )
    spread = lax.all_to_all(packed, "db", split_axis=0, concat_axis=0, tiled=True)
    places = spread[:, entries, 0, :wanted].astype(jnp.int32).reshape(holders * wanted) + middle
    places = jnp.concatenate([jnp.zeros((2,), jnp.int32), places])
    picked = pl.pallas_call(
        pick_kernel,
        out_shape=jax.ShapeDtypeStruct((holders, wanted + 2, piece, channels), jnp.bfloat16),
        in_specs=[smem, vmem],
        out_specs=vmem,
        compiler_params=small,
    )(places, spread.reshape(holders * chunks, piece, channels))
    arrived = lax.all_to_all(
        picked.reshape(holders, (wanted + 2) * piece, channels),
        "db", split_axis=0, concat_axis=0, tiled=True,
    ).reshape(holders, spans + 1, 2 * piece, channels)
    return pl.pallas_call(
        attend_kernel,
        out_shape=jax.ShapeDtypeStruct((tokens, width), jnp.bfloat16),
        in_specs=[smem] + [vmem] * 3,
        out_specs=vmem,
        compiler_params=small,
    )((me * tokens).reshape(1).astype(jnp.int32), queries, out_grad, arrived)


def solution(mesh):
    return jax.shard_map(
        body,
        mesh=mesh,
        in_specs=(
            P("db", "heads"),
            P("db", None),
            P("db", None, "heads"),
            P("db", None, "heads"),
            P("db", "heads"),
        ),
        out_specs=P("db", "heads"),
        check_vma=False,
    )
```

```python
import math

import jax
import jax.numpy as jnp
from jax import lax
from jax.experimental import pallas as pl
from jax.experimental.pallas import tpu as pltpu
from jax.sharding import PartitionSpec as P

HD = 128
GROUP = 3
SPAN = 64
LENGTH = 4096
TAIL = 16
CHUNK = 192


def pack_kernel(ids_ref, keys_ref, values_ref, out_ref, sems):
    entries, pieces = keys_ref.shape[:2]
    holders, chunks, piece, channels = out_ref.shape
    spans = ids_ref.shape[1]
    copies = []
    for e in range(entries):
        for n, ref in enumerate((keys_ref, values_ref)):
            copies.append(
                pltpu.make_async_copy(
                    ref.at[e], out_ref.at[pl.ds(n * pieces, pieces), e], sems.at[n, e]
                )
            )
    for copy in copies:
        copy.start()
    lane = lax.broadcasted_iota(jnp.int32, (piece, channels), 1)
    places = jnp.zeros((piece, channels), jnp.int32)
    for c in range(2 * spans):
        wanted_id = ids_ref[c % 2, c // 2]
        place = (wanted_id // entries) * chunks + wanted_id % entries - holders * chunks // 2
        places = jnp.where(lane == c, place, places)
    places = places.astype(jnp.float32).astype(jnp.bfloat16)
    out_ref[:, entries] = jnp.broadcast_to(places[None], (holders, piece, channels))
    for copy in copies:
        copy.wait()


def pick_kernel(index_ref, table_ref, out_ref, buffer_ref, sems):
    dests, slots = out_ref.shape[0], out_ref.shape[1] // 2
    wanted = slots - 2
    parts = sems.shape[0]
    copies = []
    for part in range(parts):
        here = pl.ds(part * (dests // parts), dests // parts)
        for d in range(here.start, here.start + here.size):
            for c in range(slots):
                buffer_ref[d, 2 * c : 2 * c + 2] = table_ref[
                    pl.ds(index_ref[d * wanted + c], 2)
                ]
        copies.append(
            pltpu.make_async_copy(buffer_ref.at[here], out_ref.at[here], sems.at[part])
        )
        copies[-1].start()
    for copy in copies:
        copy.wait()


def shift_kernel(query_ref, grad_ref, query_out_ref, grad_out_ref, wide_ref):
    tokens, width = query_ref.shape
    blocks = tokens // SPAN
    wide_ref[0:8] = jnp.zeros((8, width), jnp.float32)
    wide_ref[tokens + 8 :] = jnp.zeros((SPAN, width), jnp.float32)
    for ref, out_ref in ((query_ref, query_out_ref), (grad_ref, grad_out_ref)):
        wide_ref[8 : tokens + 8] = ref[...].astype(jnp.float32)
        for n in range(blocks + 1):
            for g in range(GROUP):
                out_ref[n, g * SPAN : (g + 1) * SPAN] = wide_ref[
                    7 + n * SPAN : 7 + (n + 1) * SPAN, g * HD : (g + 1) * HD
                ].astype(out_ref.dtype)


def soften(scores, along):
    factor = 1.0 / math.sqrt(HD)
    highest = jnp.max(scores, axis=-1, keepdims=True)
    expo = jnp.exp2((scores - highest) * (factor / math.log(2.0)))
    scale = 1.0 / jnp.sum(expo, axis=-1, keepdims=True)
    delta = jnp.sum(expo * along, axis=-1, keepdims=True) * scale
    return (expo * (along - delta)).astype(jnp.bfloat16), scale * factor


def attend_kernel(start_ref, query_ref, grad_ref, rows_ref, out_ref, result_ref, scores_ref, along_ref, slope_ref, scale_ref, sems):
    tokens = out_ref.shape[0]
    blocks = tokens // SPAN
    pieces = rows_ref.shape[0] // 2
    half_shift = tokens // 2
    start = start_ref[0]
    row = lax.broadcasted_iota(jnp.int32, (SPAN, HD), 0)
    contract = (((1,), (1,)), ((), ()))

    def height(n):
        return SPAN if n < blocks else TAIL

    def keys_of(n):
        return rows_ref[0:pieces, n].reshape(pieces * 8, HD)

    def products(n):
        values = rows_ref[pieces : 2 * pieces, n].reshape(pieces * 8, HD)
        for ref, other, out in ((query_ref, keys_of(n), scores_ref), (grad_ref, values, along_ref)):
            if n < blocks:
                rows = ref[n]
            else:
                rows = jnp.concatenate(
                    [ref[n, g * SPAN : g * SPAN + TAIL] for g in range(GROUP)], axis=0
                )
            out[n % 2, : GROUP * height(n)] = lax.dot_general(
                rows, other, contract, preferred_element_type=jnp.float32
            )

    held, copies = None, []
    products(0)
    for n in range(blocks + 1):
        if n < blocks:
            products(n + 1)
        total = GROUP * height(n)
        step = min(CHUNK, total)
        for at in range(0, total, step):
            here = slice(at, at + step)
            slope, scale = soften(scores_ref[n % 2, here], along_ref[n % 2, here])
            slope_ref[n % 2, here] = slope
            scale_ref[n % 2, here] = jnp.broadcast_to(scale, (step, HD))
        result = (
            jnp.dot(slope_ref[n % 2, :total], keys_of(n), preferred_element_type=jnp.float32)
            * scale_ref[n % 2, :total]
        )
        turned = [
            pltpu.roll(result[g * height(n) : (g + 1) * height(n)], height(n) - 1, 0)
            for g in range(GROUP)
        ]
        if n > 0:
            token = start + (n - 1) * SPAN + row
            valid = (token >= SPAN - 1) & ((token + half_shift) % LENGTH >= SPAN - 1)
            for g in range(GROUP):
                end = jnp.where(row[-8:] == SPAN - 1, turned[g][-8:], held[g][-8:])
                here = jnp.concatenate([held[g][:-8], end], axis=0)
                result_ref[(n - 1) * SPAN : n * SPAN, g * HD : (g + 1) * HD] = jnp.where(
                    valid, here, 0.0
                ).astype(out_ref.dtype)
            rows = pl.ds((n - 1) * SPAN, SPAN)
            copies.append(
                pltpu.make_async_copy(result_ref.at[rows], out_ref.at[rows], sems.at[n - 1])
            )
            copies[-1].start()
        held = turned
    for copy in copies:
        copy.wait()


def body(queries, neighbour_ids, cache_keys, cache_values, out_grad):
    holders = lax.axis_size("db")
    me = lax.axis_index("db")
    entries, entry_rows, channels = cache_keys.shape
    tokens, width = queries.shape
    spans = neighbour_ids.shape[0]
    wanted = 2 * spans
    pieces = holders // 2
    piece = entry_rows // pieces
    chunks = entries + 1
    middle = holders * chunks // 2
    vmem = pl.BlockSpec(memory_space=pltpu.VMEM)
    smem = pl.BlockSpec(memory_space=pltpu.SMEM)
    hbm = pl.BlockSpec(memory_space=pltpu.HBM)
    small = pltpu.CompilerParams(vmem_limit_bytes=16 * 2**20)

    packed = pl.pallas_call(
        pack_kernel,
        out_shape=jax.ShapeDtypeStruct((holders, chunks, piece, channels), jnp.bfloat16),
        in_specs=[smem, hbm, hbm],
        out_specs=vmem,
        scratch_shapes=[pltpu.SemaphoreType.DMA((2, entries))],
        compiler_params=small,
    )(
        neighbour_ids.T,
        *(
            pltpu.with_memory_space_constraint(
                x.reshape(entries, pieces, piece, channels), pltpu.HBM
            )
            for x in (cache_keys, cache_values)
        ),
    )
    spread = lax.all_to_all(packed, "db", split_axis=0, concat_axis=0, tiled=True)
    places = (spread[:, entries, 0, :wanted].astype(jnp.int32) + middle) * 2
    places = places.reshape(holders * wanted)
    places = jnp.concatenate([jnp.zeros((2,), jnp.int32), places])
    picked = pl.pallas_call(
        pick_kernel,
        out_shape=jax.ShapeDtypeStruct((holders, 2 * (wanted + 2), piece // 2, channels), jnp.bfloat16),
        in_specs=[smem, vmem],
        out_specs=hbm,
        scratch_shapes=[
            pltpu.VMEM((holders, 2 * (wanted + 2), piece // 2, channels), jnp.bfloat16),
            pltpu.SemaphoreType.DMA((4,)),
        ],
        compiler_params=small,
    )(places, spread.reshape(holders * chunks * 2, piece // 2, channels))
    arrived = lax.all_to_all(
        picked.reshape(holders, (wanted + 2) * piece, channels),
        "db", split_axis=0, concat_axis=0, tiled=True,
    ).reshape(holders, spans + 1, 2 * piece, channels)
    stacked = jax.ShapeDtypeStruct((spans + 1, GROUP * SPAN, HD), jnp.bfloat16)
    query_rows, grad_rows = pl.pallas_call(
        shift_kernel,
        out_shape=(stacked, stacked),
        in_specs=[vmem] * 2,
        out_specs=(vmem, vmem),
        scratch_shapes=[pltpu.VMEM((tokens + 8 + SPAN, width), jnp.float32)],
        compiler_params=small,
        cost_estimate=pl.CostEstimate(flops=10**6, bytes_accessed=4 * 10**6, transcendentals=0),
    )(queries, out_grad)
    return pl.pallas_call(
        attend_kernel,
        out_shape=jax.ShapeDtypeStruct((tokens, width), jnp.bfloat16),
        in_specs=[smem] + [vmem] * 3,
        out_specs=hbm,
        scratch_shapes=[
            pltpu.VMEM((tokens, width), jnp.bfloat16),
            pltpu.VMEM((2, GROUP * SPAN, 2 * entry_rows), jnp.float32),
            pltpu.VMEM((2, GROUP * SPAN, 2 * entry_rows), jnp.float32),
            pltpu.VMEM((2, GROUP * SPAN, 2 * entry_rows), jnp.bfloat16),
            pltpu.VMEM((2, GROUP * SPAN, HD), jnp.float32),
            pltpu.SemaphoreType.DMA((spans,)),
        ],
        compiler_params=small,
    )((me * tokens).reshape(1).astype(jnp.int32), query_rows, grad_rows, arrived)


def solution(mesh):
    return jax.shard_map(
        body,
        mesh=mesh,
        in_specs=(
            P("db", "heads"),
            P("db", None),
            P("db", None, "heads"),
            P("db", None, "heads"),
            P("db", "heads"),
        ),
        out_specs=P("db", "heads"),
        check_vma=False,
    )
```

```python
import math

import jax
import jax.numpy as jnp
from jax import lax
from jax.experimental import pallas as pl
from jax.experimental.pallas import tpu as pltpu
from jax.sharding import PartitionSpec as P

HD = 128
GROUP = 3
SPAN = 64
LENGTH = 4096
TAIL = 16
AHEAD = 3
LAG = 2
SLOTS = AHEAD + LAG + 1
LAST_AT = 0


def pack_kernel(ids_hbm_ref, keys_ref, values_ref, out_ref, ids_ref, sems, ids_sem):
    entries, pieces = keys_ref.shape[:2]
    holders, chunks, piece, channels = out_ref.shape
    spans = ids_ref.shape[1]
    ids_copy = pltpu.make_async_copy(ids_hbm_ref, ids_ref, ids_sem)
    ids_copy.start()
    copies = []
    for e in range(entries):
        for n, ref in enumerate((keys_ref, values_ref)):
            copies.append(
                pltpu.make_async_copy(
                    ref.at[e], out_ref.at[pl.ds(n * pieces, pieces), e], sems.at[n, e]
                )
            )
    for copy in copies:
        copy.start()
    ids_copy.wait()
    lane = lax.broadcasted_iota(jnp.int32, (piece, channels), 1)
    places = jnp.zeros((piece, channels), jnp.int32)
    for c in range(2 * spans):
        wanted_id = ids_ref[c % 2, c // 2]
        place = (wanted_id // entries) * chunks + wanted_id % entries - holders * chunks // 2
        places = jnp.where(lane == c, place, places)
    places = places.astype(jnp.float32).astype(jnp.bfloat16)
    out_ref[:, entries] = jnp.broadcast_to(places[None], (holders, piece, channels))
    for copy in copies:
        copy.wait()


def pick_kernel(index_ref, table_ref, out_ref, buffer_ref, sems):
    dests, slots = out_ref.shape[0], out_ref.shape[1] // 2
    wanted = slots - 2
    parts = sems.shape[0]
    copies = []
    for part in range(parts):
        here = pl.ds(part * (dests // parts), dests // parts)
        for d in range(here.start, here.start + here.size):
            for c in range(slots):
                buffer_ref[d, 2 * c : 2 * c + 2] = table_ref[
                    pl.ds(index_ref[d * wanted + c], 2)
                ]
        copies.append(
            pltpu.make_async_copy(buffer_ref.at[here], out_ref.at[here], sems.at[part])
        )
        copies[-1].start()
    for copy in copies:
        copy.wait()


def shift_kernel(query_ref, grad_ref, query_out_ref, grad_out_ref, wide_ref):
    tokens, width = query_ref.shape
    blocks = tokens // SPAN
    wide_ref[0:8] = jnp.zeros((8, width), jnp.float32)
    wide_ref[tokens + 8 :] = jnp.zeros((SPAN, width), jnp.float32)
    for ref, out_ref in ((query_ref, query_out_ref), (grad_ref, grad_out_ref)):
        wide_ref[8 : tokens + 8] = ref[...].astype(jnp.float32)
        for n in range(blocks + 1):
            for g in range(GROUP):
                out_ref[n, g * SPAN : (g + 1) * SPAN] = wide_ref[
                    7 + n * SPAN : 7 + (n + 1) * SPAN, g * HD : (g + 1) * HD
                ].astype(out_ref.dtype)


def soften(scores, along):
    factor = 1.0 / math.sqrt(HD)
    highest = jnp.max(scores, axis=-1, keepdims=True)
    expo = jnp.exp2((scores - highest) * (factor / math.log(2.0)))
    scale = 1.0 / jnp.sum(expo, axis=-1, keepdims=True)
    delta = jnp.sum(expo * along, axis=-1, keepdims=True) * scale
    return (expo * (along - delta)).astype(jnp.bfloat16), scale * factor


def attend_kernel(start_ref, query_ref, grad_ref, rows_ref, out_ref, result_ref, scores_ref, along_ref, slope_ref, scale_ref, sems):
    tokens = out_ref.shape[0]
    blocks = tokens // SPAN
    pieces = rows_ref.shape[0] // 2
    half_shift = tokens // 2
    start = start_ref[0]
    row = lax.broadcasted_iota(jnp.int32, (SPAN, HD), 0)
    contract = (((1,), (1,)), ((), ()))

    def height(n):
        return SPAN if n < blocks else TAIL

    def keys_of(n):
        return rows_ref[0:pieces, n].reshape(pieces * 8, HD)

    def products(n, slot):
        values = rows_ref[pieces : 2 * pieces, n].reshape(pieces * 8, HD)
        for ref, other, out in ((query_ref, keys_of(n), scores_ref), (grad_ref, values, along_ref)):
            if n < blocks:
                rows = ref[n]
            else:
                rows = jnp.concatenate(
                    [ref[n, g * SPAN : g * SPAN + TAIL] for g in range(GROUP)], axis=0
                )
            out[slot, : GROUP * height(n)] = lax.dot_general(
                rows, other, contract, preferred_element_type=jnp.float32
            )

    def softened(n, slot):
        total = GROUP * height(n)
        slope, scale = soften(scores_ref[slot, :total], along_ref[slot, :total])
        slope_ref[slot, :total] = slope
        scale_ref[slot, :total] = jnp.broadcast_to(scale, (total, HD))

    def finished(n, slot):
        total = GROUP * height(n)
        result = (
            jnp.dot(slope_ref[slot, :total], keys_of(n), preferred_element_type=jnp.float32)
            * scale_ref[slot, :total]
        )
        return [
            pltpu.roll(result[g * height(n) : (g + 1) * height(n)], height(n) - 1, 0)
            for g in range(GROUP)
        ]

    order = [n for n in range(blocks)]
    order.insert(LAST_AT, blocks)
    turned, copies = {}, []
    for at in range(-AHEAD, len(order) + LAG):
        if 0 <= at + AHEAD < len(order):
            products(order[at + AHEAD], (at + AHEAD) % SLOTS)
        if 0 <= at < len(order):
            softened(order[at], at % SLOTS)
        if at < LAG:
            continue
        done = order[at - LAG]
        turned[done] = finished(done, (at - LAG) % SLOTS)
        for n in range(1, blocks + 1):
            if done not in (n, n - 1) or n not in turned or n - 1 not in turned:
                continue
            token = start + (n - 1) * SPAN
            idle = (token == 0) | ((token + half_shift) % LENGTH == 0)
            kept = row >= jnp.where(idle, SPAN - 1, 0)
            for g in range(GROUP):
                before, after = turned[n - 1][g], turned[n][g]
                end = jnp.where(row[-8:] == SPAN - 1, after[-8:], before[-8:])
                here = jnp.concatenate([before[:-8], end], axis=0)
                result_ref[(n - 1) * SPAN : n * SPAN, g * HD : (g + 1) * HD] = jnp.where(
                    kept, here, 0.0
                ).astype(out_ref.dtype)
            rows = pl.ds((n - 1) * SPAN, SPAN)
            copies.append(
                pltpu.make_async_copy(result_ref.at[rows], out_ref.at[rows], sems.at[n - 1])
            )
            copies[-1].start()
    for copy in copies:
        copy.wait()


def body(queries, neighbour_ids, cache_keys, cache_values, out_grad):
    holders = lax.axis_size("db")
    me = lax.axis_index("db")
    entries, entry_rows, channels = cache_keys.shape
    tokens, width = queries.shape
    spans = neighbour_ids.shape[0]
    wanted = 2 * spans
    pieces = holders // 2
    piece = entry_rows // pieces
    chunks = entries + 1
    middle = holders * chunks // 2
    vmem = pl.BlockSpec(memory_space=pltpu.VMEM)
    smem = pl.BlockSpec(memory_space=pltpu.SMEM)
    hbm = pl.BlockSpec(memory_space=pltpu.HBM)
    small = pltpu.CompilerParams(vmem_limit_bytes=16 * 2**20)

    packed = pl.pallas_call(
        pack_kernel,
        out_shape=jax.ShapeDtypeStruct((holders, chunks, piece, channels), jnp.bfloat16),
        in_specs=[hbm] * 3,
        out_specs=vmem,
        scratch_shapes=[
            pltpu.SMEM((2, spans), jnp.int32),
            pltpu.SemaphoreType.DMA((2, entries)),
            pltpu.SemaphoreType.DMA,
        ],
        compiler_params=small,
    )(
        pltpu.with_memory_space_constraint(neighbour_ids.T, pltpu.HBM),
        *(
            pltpu.with_memory_space_constraint(
                x.reshape(entries, pieces, piece, channels), pltpu.HBM
            )
            for x in (cache_keys, cache_values)
        ),
    )
    spread = lax.all_to_all(packed, "db", split_axis=0, concat_axis=0, tiled=True)
    places = (spread[:, entries, 0, :wanted].astype(jnp.int32) + middle) * 2
    places = places.reshape(holders * wanted)
    places = jnp.concatenate([jnp.zeros((2,), jnp.int32), places])
    picked = pl.pallas_call(
        pick_kernel,
        out_shape=jax.ShapeDtypeStruct((holders, 2 * (wanted + 2), piece // 2, channels), jnp.bfloat16),
        in_specs=[smem, vmem],
        out_specs=hbm,
        scratch_shapes=[
            pltpu.VMEM((holders, 2 * (wanted + 2), piece // 2, channels), jnp.bfloat16),
            pltpu.SemaphoreType.DMA((4,)),
        ],
        compiler_params=small,
    )(places, spread.reshape(holders * chunks * 2, piece // 2, channels))
    arrived = lax.all_to_all(
        picked.reshape(holders, (wanted + 2) * piece, channels),
        "db", split_axis=0, concat_axis=0, tiled=True,
    ).reshape(holders, spans + 1, 2 * piece, channels)
    stacked = jax.ShapeDtypeStruct((spans + 1, GROUP * SPAN, HD), jnp.bfloat16)
    query_rows, grad_rows = pl.pallas_call(
        shift_kernel,
        out_shape=(stacked, stacked),
        in_specs=[vmem] * 2,
        out_specs=(vmem, vmem),
        scratch_shapes=[pltpu.VMEM((tokens + 8 + SPAN, width), jnp.float32)],
        compiler_params=small,
        cost_estimate=pl.CostEstimate(flops=10**6, bytes_accessed=4 * 10**6, transcendentals=0),
    )(queries, out_grad)
    return pl.pallas_call(
        attend_kernel,
        out_shape=jax.ShapeDtypeStruct((tokens, width), jnp.bfloat16),
        in_specs=[smem] + [vmem] * 3,
        out_specs=hbm,
        scratch_shapes=[
            pltpu.VMEM((tokens, width), jnp.bfloat16),
            pltpu.VMEM((SLOTS, GROUP * SPAN, 2 * entry_rows), jnp.float32),
            pltpu.VMEM((SLOTS, GROUP * SPAN, 2 * entry_rows), jnp.float32),
            pltpu.VMEM((SLOTS, GROUP * SPAN, 2 * entry_rows), jnp.bfloat16),
            pltpu.VMEM((SLOTS, GROUP * SPAN, HD), jnp.float32),
            pltpu.SemaphoreType.DMA((spans,)),
        ],
        compiler_params=small,
    )((me * tokens).reshape(1).astype(jnp.int32), query_rows, grad_rows, arrived)


def solution(mesh):
    return jax.shard_map(
        body,
        mesh=mesh,
        in_specs=(
            P("db", "heads"),
            P("db", None),
            P("db", None, "heads"),
            P("db", None, "heads"),
            P("db", "heads"),
        ),
        out_specs=P("db", "heads"),
        check_vma=False,
    )
```

```python
import math

import jax
import jax.numpy as jnp
from jax import lax
from jax.experimental import pallas as pl
from jax.experimental.pallas import tpu as pltpu
from jax.sharding import PartitionSpec as P

HD = 128
GROUP = 3
SPAN = 64
LENGTH = 4096
TAIL = 16
AHEAD = 3
LAG = 2
SLOTS = AHEAD + LAG + 1
LAST_AT = 0


def pack_kernel(ids_hbm_ref, keys_ref, values_ref, out_ref, ids_ref, sems, ids_sem):
    entries, pieces, halves = keys_ref.shape[:3]
    holders, chunks, rows, channels = out_ref.shape
    spans = ids_ref.shape[1]
    ids_copy = pltpu.make_async_copy(ids_hbm_ref, ids_ref, ids_sem)
    ids_copy.start()
    copies = []
    for e in range(entries):
        for n, ref in enumerate((keys_ref, values_ref)):
            copies.append(
                pltpu.make_async_copy(
                    ref.at[e],
                    out_ref.at[pl.ds(n * pieces, pieces), pl.ds(e * halves, halves)],
                    sems.at[n, e],
                )
            )
    for copy in copies:
        copy.start()
    ids_copy.wait()
    lane = lax.broadcasted_iota(jnp.int32, (rows, channels), 1)
    places = jnp.zeros((rows, channels), jnp.int32)
    for c in range(2 * spans):
        places = jnp.where(lane == c, ids_ref[c % 2, c // 2] - holders * entries // 2, places)
    places = places.astype(jnp.float32).astype(jnp.bfloat16)
    out_ref[:, chunks - 1] = jnp.broadcast_to(places[None], (holders, rows, channels))
    for copy in copies:
        copy.wait()


def pick_kernel(index_ref, table_ref, out_ref, buffer_ref, sems):
    dests, slots = out_ref.shape[0], out_ref.shape[1] // 2
    wanted = slots - 2
    parts = sems.shape[0]
    copies = []
    for part in range(parts):
        here = pl.ds(part * (dests // parts), dests // parts)
        for d in range(here.start, here.start + here.size):
            for c in range(slots):
                buffer_ref[d, 2 * c : 2 * c + 2] = table_ref[
                    pl.ds(index_ref[d * wanted + c], 2)
                ]
        copies.append(
            pltpu.make_async_copy(buffer_ref.at[here], out_ref.at[here], sems.at[part])
        )
        copies[-1].start()
    for copy in copies:
        copy.wait()


def shift_kernel(query_ref, grad_ref, query_out_ref, grad_out_ref, wide_ref):
    tokens, width = query_ref.shape
    blocks = tokens // SPAN
    wide_ref[0:8] = jnp.zeros((8, width), jnp.float32)
    wide_ref[tokens + 8 :] = jnp.zeros((SPAN, width), jnp.float32)
    for ref, out_ref in ((query_ref, query_out_ref), (grad_ref, grad_out_ref)):
        wide_ref[8 : tokens + 8] = ref[...].astype(jnp.float32)
        for n in range(blocks + 1):
            for g in range(GROUP):
                out_ref[n, g * SPAN : (g + 1) * SPAN] = wide_ref[
                    7 + n * SPAN : 7 + (n + 1) * SPAN, g * HD : (g + 1) * HD
                ].astype(out_ref.dtype)


def soften(scores, along):
    factor = 1.0 / math.sqrt(HD)
    highest = jnp.max(scores, axis=-1, keepdims=True)
    expo = jnp.exp2((scores - highest) * (factor / math.log(2.0)))
    scale = 1.0 / jnp.sum(expo, axis=-1, keepdims=True)
    delta = jnp.sum(expo * along, axis=-1, keepdims=True) * scale
    return (expo * (along - delta)).astype(jnp.bfloat16), scale * factor


def attend_kernel(start_ref, query_ref, grad_ref, rows_ref, out_ref, result_ref, scores_ref, along_ref, slope_ref, scale_ref, sems):
    tokens = out_ref.shape[0]
    blocks = tokens // SPAN
    pieces = rows_ref.shape[0] // 2
    half_shift = tokens // 2
    start = start_ref[0]
    row = lax.broadcasted_iota(jnp.int32, (SPAN, HD), 0)
    contract = (((1,), (1,)), ((), ()))

    def height(n):
        return SPAN if n < blocks else TAIL

    def keys_of(n):
        return rows_ref[0:pieces, n].reshape(pieces * 8, HD)

    def products(n, slot):
        values = rows_ref[pieces : 2 * pieces, n].reshape(pieces * 8, HD)
        for ref, other, out in ((query_ref, keys_of(n), scores_ref), (grad_ref, values, along_ref)):
            if n < blocks:
                rows = ref[n]
            else:
                rows = jnp.concatenate(
                    [ref[n, g * SPAN : g * SPAN + TAIL] for g in range(GROUP)], axis=0
                )
            out[slot, : GROUP * height(n)] = lax.dot_general(
                rows, other, contract, preferred_element_type=jnp.float32
            )

    def softened(n, slot):
        total = GROUP * height(n)
        slope, scale = soften(scores_ref[slot, :total], along_ref[slot, :total])
        slope_ref[slot, :total] = slope
        scale_ref[slot, :total] = jnp.broadcast_to(scale, (total, HD))

    def finished(n, slot):
        total = GROUP * height(n)
        result = (
            jnp.dot(slope_ref[slot, :total], keys_of(n), preferred_element_type=jnp.float32)
            * scale_ref[slot, :total]
        )
        return [
            pltpu.roll(result[g * height(n) : (g + 1) * height(n)], height(n) - 1, 0)
            for g in range(GROUP)
        ]

    order = [n for n in range(blocks)]
    order.insert(LAST_AT, blocks)
    turned, copies = {}, []
    for at in range(-AHEAD, len(order) + LAG):
        if 0 <= at + AHEAD < len(order):
            products(order[at + AHEAD], (at + AHEAD) % SLOTS)
        if 0 <= at < len(order):
            softened(order[at], at % SLOTS)
        if at < LAG:
            continue
        done = order[at - LAG]
        turned[done] = finished(done, (at - LAG) % SLOTS)
        for n in range(1, blocks + 1):
            if done not in (n, n - 1) or n not in turned or n - 1 not in turned:
                continue
            token = start + (n - 1) * SPAN
            idle = (token == 0) | ((token + half_shift) % LENGTH == 0)
            kept = row >= jnp.where(idle, SPAN - 1, 0)
            for g in range(GROUP):
                before, after = turned[n - 1][g], turned[n][g]
                end = jnp.where(row[-8:] == SPAN - 1, after[-8:], before[-8:])
                here = jnp.concatenate([before[:-8], end], axis=0)
                result_ref[(n - 1) * SPAN : n * SPAN, g * HD : (g + 1) * HD] = jnp.where(
                    kept, here, 0.0
                ).astype(out_ref.dtype)
            rows = pl.ds((n - 1) * SPAN, SPAN)
            copies.append(
                pltpu.make_async_copy(result_ref.at[rows], out_ref.at[rows], sems.at[n - 1])
            )
            copies[-1].start()
    for copy in copies:
        copy.wait()


def body(queries, neighbour_ids, cache_keys, cache_values, out_grad):
    holders = lax.axis_size("db")
    me = lax.axis_index("db")
    entries, entry_rows, channels = cache_keys.shape
    tokens, width = queries.shape
    spans = neighbour_ids.shape[0]
    wanted = 2 * spans
    pieces = holders // 2
    piece = entry_rows // pieces
    rows = 2
    halves = piece // rows
    chunks = entries * halves + 1
    vmem = pl.BlockSpec(memory_space=pltpu.VMEM)
    smem = pl.BlockSpec(memory_space=pltpu.SMEM)
    hbm = pl.BlockSpec(memory_space=pltpu.HBM)
    small = pltpu.CompilerParams(vmem_limit_bytes=16 * 2**20)

    packed = pl.pallas_call(
        pack_kernel,
        out_shape=jax.ShapeDtypeStruct((holders, chunks, rows, channels), jnp.bfloat16),
        in_specs=[hbm] * 3,
        out_specs=vmem,
        scratch_shapes=[
            pltpu.SMEM((2, spans), jnp.int32),
            pltpu.SemaphoreType.DMA((2, entries)),
            pltpu.SemaphoreType.DMA,
        ],
        compiler_params=small,
    )(
        pltpu.with_memory_space_constraint(neighbour_ids.T, pltpu.HBM),
        *(
            pltpu.with_memory_space_constraint(
                x.reshape(entries, pieces, halves, rows, channels), pltpu.HBM
            )
            for x in (cache_keys, cache_values)
        ),
    )
    spread = lax.all_to_all(packed, "db", split_axis=0, concat_axis=0, tiled=True)
    ids = spread[:, chunks - 1, 0, :wanted].astype(jnp.int32) + holders * entries // 2
    places = (ids * halves + lax.div(ids, entries)).reshape(holders * wanted)
    places = jnp.concatenate([jnp.zeros((2,), jnp.int32), places])
    picked = pl.pallas_call(
        pick_kernel,
        out_shape=jax.ShapeDtypeStruct((holders, halves * (wanted + 2), rows, channels), jnp.bfloat16),
        in_specs=[smem, vmem],
        out_specs=hbm,
        scratch_shapes=[
            pltpu.VMEM((holders, halves * (wanted + 2), rows, channels), jnp.bfloat16),
            pltpu.SemaphoreType.DMA((4,)),
        ],
        compiler_params=small,
    )(places, spread.reshape(holders * chunks, rows, channels))
    arrived = lax.all_to_all(
        picked.reshape(holders, (wanted + 2) * piece, channels),
        "db", split_axis=0, concat_axis=0, tiled=True,
    ).reshape(holders, spans + 1, 2 * piece, channels)
    stacked = jax.ShapeDtypeStruct((spans + 1, GROUP * SPAN, HD), jnp.bfloat16)
    query_rows, grad_rows = pl.pallas_call(
        shift_kernel,
        out_shape=(stacked, stacked),
        in_specs=[vmem] * 2,
        out_specs=(vmem, vmem),
        scratch_shapes=[pltpu.VMEM((tokens + 8 + SPAN, width), jnp.float32)],
        compiler_params=small,
        cost_estimate=pl.CostEstimate(flops=10**6, bytes_accessed=4 * 10**6, transcendentals=0),
    )(queries, out_grad)
    return pl.pallas_call(
        attend_kernel,
        out_shape=jax.ShapeDtypeStruct((tokens, width), jnp.bfloat16),
        in_specs=[smem] + [vmem] * 3,
        out_specs=hbm,
        scratch_shapes=[
            pltpu.VMEM((tokens, width), jnp.bfloat16),
            pltpu.VMEM((SLOTS, GROUP * SPAN, 2 * entry_rows), jnp.float32),
            pltpu.VMEM((SLOTS, GROUP * SPAN, 2 * entry_rows), jnp.float32),
            pltpu.VMEM((SLOTS, GROUP * SPAN, 2 * entry_rows), jnp.bfloat16),
            pltpu.VMEM((SLOTS, GROUP * SPAN, HD), jnp.float32),
            pltpu.SemaphoreType.DMA((spans,)),
        ],
        compiler_params=small,
    )((me * tokens).reshape(1).astype(jnp.int32), query_rows, grad_rows, arrived)


def solution(mesh):
    return jax.shard_map(
        body,
        mesh=mesh,
        in_specs=(
            P("db", "heads"),
            P("db", None),
            P("db", None, "heads"),
            P("db", None, "heads"),
            P("db", "heads"),
        ),
        out_specs=P("db", "heads"),
        check_vma=False,
    )
```

```python
import functools
import math

import jax
import jax.numpy as jnp
from jax import lax
from jax.experimental import pallas as pl
from jax.experimental.pallas import tpu as pltpu
from jax.sharding import PartitionSpec as P

HD = 128
GROUP = 3
SPAN = 64
LENGTH = 4096
TAIL = 8
AHEAD = 3
LAG = 2
SLOTS = AHEAD + LAG + 1
LAST_AT = 0


def exchange_order(holders):
    side = math.isqrt(holders)
    assert side * side == holders and side % 2 == 0
    along_z = [a // 2 + side // 2 * (a % 2) for a in range(side)]
    return [y * side + z for z in along_z for y in range(side)]


def place_of(holder, holders):
    side = math.isqrt(holders)
    y, z = lax.div(holder, side), lax.rem(holder, side)
    return (2 * lax.rem(z, side // 2) + lax.div(z, side // 2)) * side + y


def pack_kernel(_, ids_hbm_ref, keys_ref, values_ref, out_ref, ids_ref, sems, ids_sem):
    entries, pieces, halves = keys_ref.shape[:3]
    holders, chunks, rows, channels = out_ref.shape
    spans = ids_ref.shape[1]
    ids_copy = pltpu.make_async_copy(ids_hbm_ref, ids_ref, ids_sem)
    ids_copy.start()
    copies = []
    for e in range(entries):
        for n, ref in enumerate((keys_ref, values_ref)):
            copies.append(
                pltpu.make_async_copy(
                    ref.at[e],
                    out_ref.at[pl.ds(n * pieces, pieces), pl.ds(e * halves, halves)],
                    sems.at[n, e],
                )
            )
    for copy in copies:
        copy.start()
    ids_copy.wait()
    lane = lax.broadcasted_iota(jnp.int32, (rows, channels), 1)
    places = jnp.zeros((rows, channels), jnp.int32)
    for c in range(2 * spans):
        wanted_id = ids_ref[c % 2, c // 2]
        place = place_of(lax.div(wanted_id, entries), holders) * entries
        place = place + lax.rem(wanted_id, entries) - holders * entries // 2
        places = jnp.where(lane == c, place, places)
    places = places.astype(jnp.float32).astype(jnp.bfloat16)
    out_ref[:, chunks - 1] = jnp.broadcast_to(places[None], (holders, rows, channels))
    for copy in copies:
        copy.wait()


def pick_kernel(order, index_ref, table_ref, out_ref):
    dests, slots = out_ref.shape[0], out_ref.shape[1] // 2
    wanted = slots - 2
    for d in range(dests):
        before = order.index(order[d] - 1) if order[d] > 0 else d
        sources = [before * wanted + wanted - 2 + c for c in range(2)]
        sources += [d * wanted + c for c in range(wanted)]
        for c, source in enumerate(sources):
            out_ref[d, 2 * c : 2 * c + 2] = table_ref[pl.ds(index_ref[source], 2)]


def soften(scores, along):
    factor = 1.0 / math.sqrt(HD)
    highest = jnp.max(scores, axis=-1, keepdims=True)
    expo = jnp.exp2((scores - highest) * (factor / math.log(2.0)))
    scale = 1.0 / jnp.sum(expo, axis=-1, keepdims=True)
    delta = jnp.sum(expo * along, axis=-1, keepdims=True) * scale
    return (expo * (along - delta)).astype(jnp.bfloat16), scale * factor


def attend_kernel(start_ref, query_ref, grad_ref, rows_ref, out_ref, result_ref, scores_ref, along_ref, slope_ref, scale_ref, sems):
    tokens = out_ref.shape[0]
    blocks = tokens // SPAN
    pieces = rows_ref.shape[0] // 2
    half_shift = tokens // 2
    start = start_ref[0]
    row = lax.broadcasted_iota(jnp.int32, (SPAN, HD), 0)
    contract = (((1,), (1,)), ((), ()))

    def keys_of(n):
        return rows_ref[0:pieces, n].reshape(pieces * 8, HD)

    def parts(n):
        own = [(n * SPAN, (n + 1) * SPAN)] if n < blocks else []
        end = [(n * SPAN - TAIL, n * SPAN)] if n > 0 else []
        return own + end

    def height(n):
        return GROUP * sum(b - a for a, b in parts(n))

    def products(n, slot):
        values = rows_ref[pieces : 2 * pieces, n].reshape(pieces * 8, HD)
        for ref, other, out in ((query_ref, keys_of(n), scores_ref), (grad_ref, values, along_ref)):
            rows = [
                ref[a:b, g * HD : (g + 1) * HD] for a, b in parts(n) for g in range(GROUP)
            ]
            out[slot, : height(n)] = lax.dot_general(
                jnp.concatenate(rows, axis=0), other, contract, preferred_element_type=jnp.float32
            )

    def softened(n, slot):
        total = height(n)
        slope, scale = soften(scores_ref[slot, :total], along_ref[slot, :total])
        slope_ref[slot, :total] = slope
        scale_ref[slot, :total] = jnp.broadcast_to(scale, (total, HD))

    def finished(n, slot):
        total = height(n)
        result = (
            jnp.dot(slope_ref[slot, :total], keys_of(n), preferred_element_type=jnp.float32)
            * scale_ref[slot, :total]
        )
        split, at = [], 0
        for a, b in parts(n):
            split.append([result[at + g * (b - a) : at + (g + 1) * (b - a)] for g in range(GROUP)])
            at += GROUP * (b - a)
        return split

    order = [n for n in range(blocks)]
    order.insert(LAST_AT, blocks)
    done_of, copies = {}, []
    for at in range(-AHEAD, len(order) + LAG):
        if 0 <= at + AHEAD < len(order):
            products(order[at + AHEAD], (at + AHEAD) % SLOTS)
        if 0 <= at < len(order):
            softened(order[at], at % SLOTS)
        if at < LAG:
            continue
        done = order[at - LAG]
        done_of[done] = finished(done, (at - LAG) % SLOTS)
        for n in range(1, blocks + 1):
            if done not in (n, n - 1) or n not in done_of or n - 1 not in done_of:
                continue
            token = start + (n - 1) * SPAN
            idle = (token == 0) | ((token + half_shift) % LENGTH == 0)
            kept = row >= jnp.where(idle, SPAN - 1, 0)
            for g in range(GROUP):
                before, after = done_of[n - 1][0][g], done_of[n][-1][g]
                end = jnp.where(row[-8:] == SPAN - 1, after[-8:], before[-8:])
                here = jnp.concatenate([before[:-8], end], axis=0)
                result_ref[(n - 1) * SPAN : n * SPAN, g * HD : (g + 1) * HD] = jnp.where(
                    kept, here, 0.0
                ).astype(out_ref.dtype)
            rows = pl.ds((n - 1) * SPAN, SPAN)
            copies.append(
                pltpu.make_async_copy(result_ref.at[rows], out_ref.at[rows], sems.at[n - 1])
            )
            copies[-1].start()
    for copy in copies:
        copy.wait()


def body(queries, neighbour_ids, cache_keys, cache_values, out_grad):
    holders = lax.axis_size("db")
    me = lax.axis_index("db")
    entries, entry_rows, channels = cache_keys.shape
    tokens, width = queries.shape
    spans = neighbour_ids.shape[0]
    wanted = 2 * spans
    pieces = holders // 2
    piece = entry_rows // pieces
    rows = 2
    halves = piece // rows
    chunks = entries * halves + 1
    order = exchange_order(holders)
    vmem = pl.BlockSpec(memory_space=pltpu.VMEM)
    smem = pl.BlockSpec(memory_space=pltpu.SMEM)
    hbm = pl.BlockSpec(memory_space=pltpu.HBM)
    small = pltpu.CompilerParams(vmem_limit_bytes=16 * 2**20)

    start = (me * tokens).reshape(1).astype(jnp.int32)
    packed = pl.pallas_call(
        pack_kernel,
        out_shape=jax.ShapeDtypeStruct((holders, chunks, rows, channels), jnp.bfloat16),
        in_specs=[smem] + [hbm] * 3,
        out_specs=vmem,
        scratch_shapes=[
            pltpu.SMEM((2, spans), jnp.int32),
            pltpu.SemaphoreType.DMA((2, entries)),
            pltpu.SemaphoreType.DMA,
        ],
        compiler_params=small,
    )(
        start,
        pltpu.with_memory_space_constraint(neighbour_ids.T, pltpu.HBM),
        *(
            pltpu.with_memory_space_constraint(
                x.reshape(entries, pieces, halves, rows, channels), pltpu.HBM
            )
            for x in (cache_keys, cache_values)
        ),
    )
    exchange = functools.partial(
        lax.all_to_all, axis_name="db", split_axis=0, concat_axis=0, tiled=True, axis_index_groups=[order]
    )
    spread = exchange(packed)
    ids = spread[:, chunks - 1, 0, :wanted].astype(jnp.int32) + holders * entries // 2
    places = (ids * halves + lax.div(ids, entries)).reshape(holders * wanted)
    picked = pl.pallas_call(
        functools.partial(pick_kernel, order),
        out_shape=jax.ShapeDtypeStruct((holders, halves * (wanted + 2), rows, channels), jnp.bfloat16),
        in_specs=[smem, vmem],
        out_specs=vmem,
        compiler_params=small,
    )(places, spread.reshape(holders * chunks, rows, channels))
    arrived = exchange(picked.reshape(holders, (wanted + 2) * piece, channels)).reshape(
        holders, spans + 1, 2 * piece, channels
    )
    return pl.pallas_call(
        attend_kernel,
        out_shape=jax.ShapeDtypeStruct((tokens, width), jnp.bfloat16),
        in_specs=[smem] + [vmem] * 3,
        out_specs=hbm,
        scratch_shapes=[
            pltpu.VMEM((tokens, width), jnp.bfloat16),
            pltpu.VMEM((SLOTS, GROUP * (SPAN + TAIL), 2 * entry_rows), jnp.float32),
            pltpu.VMEM((SLOTS, GROUP * (SPAN + TAIL), 2 * entry_rows), jnp.float32),
            pltpu.VMEM((SLOTS, GROUP * (SPAN + TAIL), 2 * entry_rows), jnp.bfloat16),
            pltpu.VMEM((SLOTS, GROUP * (SPAN + TAIL), HD), jnp.float32),
            pltpu.SemaphoreType.DMA((spans,)),
        ],
        compiler_params=small,
    )(start, queries, out_grad, arrived)


def solution(mesh):
    return jax.shard_map(
        body,
        mesh=mesh,
        in_specs=(
            P("db", "heads"),
            P("db", None),
            P("db", None, "heads"),
            P("db", None, "heads"),
            P("db", "heads"),
        ),
        out_specs=P("db", "heads"),
        check_vma=False,
    )
```

```python
import functools
import math

import jax
import jax.numpy as jnp
from jax import lax
from jax.experimental import pallas as pl
from jax.experimental.pallas import tpu as pltpu
from jax.sharding import PartitionSpec as P

HD = 128
GROUP = 3
SPAN = 64
LENGTH = 4096
TAIL = 8
AHEAD = 3
LAG = 2
SLOTS = AHEAD + LAG + 1
LAST_AT = 0


def exchange_order(holders):
    side = math.isqrt(holders)
    half = side // 2
    assert side * side == holders and side == 2 * half
    along_z = [a // 2 + half * ((a + 1) % 2) for a in range(side)]
    return [(b + half) % side * side + z for z in along_z for b in range(side)]


def place_of(holder, holders):
    side = math.isqrt(holders)
    half = side // 2
    y, z = lax.div(holder, side), lax.rem(holder, side)
    return (2 * lax.rem(z, half) + 1 - lax.div(z, half)) * side + lax.rem(y + half, side)


def pack_kernel(_, ids_hbm_ref, keys_ref, values_ref, out_ref, ids_ref, sems, ids_sem):
    entries, pieces, halves = keys_ref.shape[:3]
    holders, chunks, rows, channels = out_ref.shape
    spans = ids_ref.shape[1]
    ids_copy = pltpu.make_async_copy(ids_hbm_ref, ids_ref, ids_sem)
    ids_copy.start()
    copies = []
    for e in range(entries):
        for n, ref in enumerate((keys_ref, values_ref)):
            copies.append(
                pltpu.make_async_copy(
                    ref.at[e],
                    out_ref.at[pl.ds(n * pieces, pieces), pl.ds(e * halves, halves)],
                    sems.at[n, e],
                )
            )
    for copy in copies:
        copy.start()
    ids_copy.wait()
    lane = lax.broadcasted_iota(jnp.int32, (rows, channels), 1)
    places = jnp.zeros((rows, channels), jnp.int32)
    for c in range(2 * spans):
        wanted_id = ids_ref[c % 2, c // 2]
        place = place_of(lax.div(wanted_id, entries), holders) * entries
        place = place + lax.rem(wanted_id, entries) - holders * entries // 2
        places = jnp.where(lane == c, place, places)
    places = places.astype(jnp.float32).astype(jnp.bfloat16)
    out_ref[:, chunks - 1] = jnp.broadcast_to(places[None], (holders, rows, channels))
    for copy in copies:
        copy.wait()


def pick_kernel(order, index_ref, table_ref, out_ref):
    dests, slots = out_ref.shape[0], out_ref.shape[1] // 2
    wanted = slots - 2
    for d in range(dests):
        before = order.index(order[d] - 1) if order[d] > 0 else d
        sources = [before * wanted + wanted - 2 + c for c in range(2)]
        sources += [d * wanted + c for c in range(wanted)]
        for c, source in enumerate(sources):
            out_ref[d, 2 * c : 2 * c + 2] = table_ref[pl.ds(index_ref[source], 2)]


def soften(scores, along):
    factor = 1.0 / math.sqrt(HD)
    highest = jnp.max(scores, axis=-1, keepdims=True)
    expo = jnp.exp2((scores - highest) * (factor / math.log(2.0)))
    scale = 1.0 / jnp.sum(expo, axis=-1, keepdims=True)
    delta = jnp.sum(expo * along, axis=-1, keepdims=True) * scale
    return (expo * (along - delta)).astype(jnp.bfloat16), scale * factor


def attend_kernel(start_ref, query_ref, grad_ref, rows_ref, out_ref, result_ref, scores_ref, along_ref, slope_ref, scale_ref, sems):
    tokens = out_ref.shape[0]
    blocks = tokens // SPAN
    pieces = rows_ref.shape[0] // 2
    half_shift = tokens // 2
    start = start_ref[0]
    row = lax.broadcasted_iota(jnp.int32, (SPAN, HD), 0)
    contract = (((1,), (1,)), ((), ()))

    def keys_of(n):
        return rows_ref[0:pieces, n].reshape(pieces * 8, HD)

    def parts(n):
        own = [(n * SPAN, (n + 1) * SPAN)] if n < blocks else []
        end = [(n * SPAN - TAIL, n * SPAN)] if n > 0 else []
        return own + end

    def height(n):
        return GROUP * sum(b - a for a, b in parts(n))

    def products(n, slot):
        values = rows_ref[pieces : 2 * pieces, n].reshape(pieces * 8, HD)
        for ref, other, out in ((query_ref, keys_of(n), scores_ref), (grad_ref, values, along_ref)):
            rows = [
                ref[a:b, g * HD : (g + 1) * HD] for a, b in parts(n) for g in range(GROUP)
            ]
            out[slot, : height(n)] = lax.dot_general(
                jnp.concatenate(rows, axis=0), other, contract, preferred_element_type=jnp.float32
            )

    def softened(n, slot):
        total = height(n)
        slope, scale = soften(scores_ref[slot, :total], along_ref[slot, :total])
        slope_ref[slot, :total] = slope
        scale_ref[slot, :total] = jnp.broadcast_to(scale, (total, HD))

    def finished(n, slot):
        total = height(n)
        result = (
            jnp.dot(slope_ref[slot, :total], keys_of(n), preferred_element_type=jnp.float32)
            * scale_ref[slot, :total]
        )
        split, at = [], 0
        for a, b in parts(n):
            split.append([result[at + g * (b - a) : at + (g + 1) * (b - a)] for g in range(GROUP)])
            at += GROUP * (b - a)
        return split

    order = [n for n in range(blocks)]
    order.insert(LAST_AT, blocks)
    done_of, copies = {}, []
    for at in range(-AHEAD, len(order) + LAG):
        if 0 <= at + AHEAD < len(order):
            products(order[at + AHEAD], (at + AHEAD) % SLOTS)
        if 0 <= at < len(order):
            softened(order[at], at % SLOTS)
        if at < LAG:
            continue
        done = order[at - LAG]
        done_of[done] = finished(done, (at - LAG) % SLOTS)
        for n in range(1, blocks + 1):
            if done not in (n, n - 1) or n not in done_of or n - 1 not in done_of:
                continue
            token = start + (n - 1) * SPAN
            idle = (token == 0) | ((token + half_shift) % LENGTH == 0)
            kept = row >= jnp.where(idle, SPAN - 1, 0)
            for g in range(GROUP):
                before, after = done_of[n - 1][0][g], done_of[n][-1][g]
                end = jnp.where(row[-8:] == SPAN - 1, after[-8:], before[-8:])
                here = jnp.concatenate([before[:-8], end], axis=0)
                result_ref[(n - 1) * SPAN : n * SPAN, g * HD : (g + 1) * HD] = jnp.where(
                    kept, here, 0.0
                ).astype(out_ref.dtype)
            rows = pl.ds((n - 1) * SPAN, SPAN)
            copies.append(
                pltpu.make_async_copy(result_ref.at[rows], out_ref.at[rows], sems.at[n - 1])
            )
            copies[-1].start()
    for copy in copies:
        copy.wait()


def body(queries, neighbour_ids, cache_keys, cache_values, out_grad):
    holders = lax.axis_size("db")
    me = lax.axis_index("db")
    entries, entry_rows, channels = cache_keys.shape
    tokens, width = queries.shape
    spans = neighbour_ids.shape[0]
    wanted = 2 * spans
    pieces = holders // 2
    piece = entry_rows // pieces
    rows = 2
    halves = piece // rows
    chunks = entries * halves + 1
    order = exchange_order(holders)
    vmem = pl.BlockSpec(memory_space=pltpu.VMEM)
    smem = pl.BlockSpec(memory_space=pltpu.SMEM)
    hbm = pl.BlockSpec(memory_space=pltpu.HBM)
    small = pltpu.CompilerParams(vmem_limit_bytes=16 * 2**20)

    start = (me * tokens).reshape(1).astype(jnp.int32)
    packed = pl.pallas_call(
        pack_kernel,
        out_shape=jax.ShapeDtypeStruct((holders, chunks, rows, channels), jnp.bfloat16),
        in_specs=[smem] + [hbm] * 3,
        out_specs=vmem,
        scratch_shapes=[
            pltpu.SMEM((2, spans), jnp.int32),
            pltpu.SemaphoreType.DMA((2, entries)),
            pltpu.SemaphoreType.DMA,
        ],
        compiler_params=small,
    )(
        start,
        pltpu.with_memory_space_constraint(neighbour_ids.T, pltpu.HBM),
        *(
            pltpu.with_memory_space_constraint(
                x.reshape(entries, pieces, halves, rows, channels), pltpu.HBM
            )
            for x in (cache_keys, cache_values)
        ),
    )
    exchange = functools.partial(
        lax.all_to_all, axis_name="db", split_axis=0, concat_axis=0, tiled=True, axis_index_groups=[order]
    )
    spread = exchange(packed)
    ids = spread[:, chunks - 1, 0, :wanted].astype(jnp.int32) + holders * entries // 2
    places = (ids * halves + lax.div(ids, entries)).reshape(holders * wanted)
    picked = pl.pallas_call(
        functools.partial(pick_kernel, order),
        out_shape=jax.ShapeDtypeStruct((holders, halves * (wanted + 2), rows, channels), jnp.bfloat16),
        in_specs=[smem, vmem],
        out_specs=vmem,
        compiler_params=small,
    )(places, spread.reshape(holders * chunks, rows, channels))
    arrived = exchange(picked.reshape(holders, (wanted + 2) * piece, channels)).reshape(
        holders, spans + 1, 2 * piece, channels
    )
    return pl.pallas_call(
        attend_kernel,
        out_shape=jax.ShapeDtypeStruct((tokens, width), jnp.bfloat16),
        in_specs=[smem] + [vmem] * 3,
        out_specs=hbm,
        scratch_shapes=[
            pltpu.VMEM((tokens, width), jnp.bfloat16),
            pltpu.VMEM((SLOTS, GROUP * (SPAN + TAIL), 2 * entry_rows), jnp.float32),
            pltpu.VMEM((SLOTS, GROUP * (SPAN + TAIL), 2 * entry_rows), jnp.float32),
            pltpu.VMEM((SLOTS, GROUP * (SPAN + TAIL), 2 * entry_rows), jnp.bfloat16),
            pltpu.VMEM((SLOTS, GROUP * (SPAN + TAIL), HD), jnp.float32),
            pltpu.SemaphoreType.DMA((spans,)),
        ],
        compiler_params=small,
    )(start, queries, out_grad, arrived)


def solution(mesh):
    return jax.shard_map(
        body,
        mesh=mesh,
        in_specs=(
            P("db", "heads"),
            P("db", None),
            P("db", None, "heads"),
            P("db", None, "heads"),
            P("db", "heads"),
        ),
        out_specs=P("db", "heads"),
        check_vma=False,
    )
```

```python
import functools
import math

import jax
import jax.numpy as jnp
from jax import lax
from jax.experimental import pallas as pl
from jax.experimental.pallas import tpu as pltpu
from jax.sharding import PartitionSpec as P

HD = 128
GROUP = 3
SPAN = 64
LENGTH = 4096
TAIL = 8
AHEAD = 3
LAG = 2
SLOTS = AHEAD + LAG + 1
LAST_AT = 0


def exchange_order(holders):
    side = math.isqrt(holders)
    half = side // 2
    assert side * side == holders and side == 2 * half
    along_z = [(a // 2 + half * (a % 2) + side - 2) % side for a in range(side)]
    return [(b + half) % side * side + z for z in along_z for b in range(side)]


def place_of(holder, holders):
    side = math.isqrt(holders)
    half = side // 2
    y, z = lax.div(holder, side), lax.rem(holder + 2, side)
    return (2 * lax.rem(z, half) + lax.div(z, half)) * side + lax.rem(y + half, side)


def pack_kernel(_, ids_hbm_ref, keys_ref, values_ref, out_ref, ids_ref, sems, ids_sem):
    entries, pieces, halves = keys_ref.shape[:3]
    holders, chunks, rows, channels = out_ref.shape
    spans = ids_ref.shape[1]
    ids_copy = pltpu.make_async_copy(ids_hbm_ref, ids_ref, ids_sem)
    ids_copy.start()
    copies = []
    for e in range(entries):
        for n, ref in enumerate((keys_ref, values_ref)):
            copies.append(
                pltpu.make_async_copy(
                    ref.at[e],
                    out_ref.at[pl.ds(n * pieces, pieces), pl.ds(e * halves, halves)],
                    sems.at[n, e],
                )
            )
    for copy in copies:
        copy.start()
    ids_copy.wait()
    lane = lax.broadcasted_iota(jnp.int32, (rows, channels), 1)
    places = jnp.zeros((rows, channels), jnp.int32)
    for c in range(2 * spans):
        wanted_id = ids_ref[c % 2, c // 2]
        place = place_of(lax.div(wanted_id, entries), holders) * entries
        place = place + lax.rem(wanted_id, entries) - holders * entries // 2
        places = jnp.where(lane == c, place, places)
    places = places.astype(jnp.float32).astype(jnp.bfloat16)
    out_ref[:, chunks - 1] = jnp.broadcast_to(places[None], (holders, rows, channels))
    for copy in copies:
        copy.wait()


def pick_kernel(order, index_ref, table_ref, out_ref):
    dests, slots = out_ref.shape[0], out_ref.shape[1] // 2
    wanted = slots - 2
    for d in range(dests):
        before = order.index(order[d] - 1) if order[d] > 0 else d
        sources = [before * wanted + wanted - 2 + c for c in range(2)]
        sources += [d * wanted + c for c in range(wanted)]
        for c, source in enumerate(sources):
            out_ref[d, 2 * c : 2 * c + 2] = table_ref[pl.ds(index_ref[source], 2)]


def soften(scores, along):
    factor = 1.0 / math.sqrt(HD)
    highest = jnp.max(scores, axis=-1, keepdims=True)
    expo = jnp.exp2((scores - highest) * (factor / math.log(2.0)))
    scale = 1.0 / jnp.sum(expo, axis=-1, keepdims=True)
    delta = jnp.sum(expo * along, axis=-1, keepdims=True) * scale
    return (expo * (along - delta)).astype(jnp.bfloat16), scale * factor


def attend_kernel(start_ref, query_ref, grad_ref, rows_ref, out_ref, result_ref, scores_ref, along_ref, slope_ref, scale_ref, sems):
    tokens = out_ref.shape[0]
    blocks = tokens // SPAN
    pieces = rows_ref.shape[0] // 2
    half_shift = tokens // 2
    start = start_ref[0]
    row = lax.broadcasted_iota(jnp.int32, (SPAN, HD), 0)
    contract = (((1,), (1,)), ((), ()))

    def keys_of(n):
        return rows_ref[0:pieces, n].reshape(pieces * 8, HD)

    def parts(n):
        own = [(n * SPAN, (n + 1) * SPAN)] if n < blocks else []
        end = [(n * SPAN - TAIL, n * SPAN)] if n > 0 else []
        return own + end

    def height(n):
        return GROUP * sum(b - a for a, b in parts(n))

    def products(n, slot):
        values = rows_ref[pieces : 2 * pieces, n].reshape(pieces * 8, HD)
        for ref, other, out in ((query_ref, keys_of(n), scores_ref), (grad_ref, values, along_ref)):
            rows = [
                ref[a:b, g * HD : (g + 1) * HD] for a, b in parts(n) for g in range(GROUP)
            ]
            out[slot, : height(n)] = lax.dot_general(
                jnp.concatenate(rows, axis=0), other, contract, preferred_element_type=jnp.float32
            )

    def softened(n, slot):
        total = height(n)
        slope, scale = soften(scores_ref[slot, :total], along_ref[slot, :total])
        slope_ref[slot, :total] = slope
        scale_ref[slot, :total] = jnp.broadcast_to(scale, (total, HD))

    def finished(n, slot):
        total = height(n)
        result = (
            jnp.dot(slope_ref[slot, :total], keys_of(n), preferred_element_type=jnp.float32)
            * scale_ref[slot, :total]
        )
        split, at = [], 0
        for a, b in parts(n):
            split.append([result[at + g * (b - a) : at + (g + 1) * (b - a)] for g in range(GROUP)])
            at += GROUP * (b - a)
        return split

    order = [n for n in range(blocks)]
    order.insert(LAST_AT, blocks)
    done_of, copies = {}, []
    for at in range(-AHEAD, len(order) + LAG):
        if 0 <= at + AHEAD < len(order):
            products(order[at + AHEAD], (at + AHEAD) % SLOTS)
        if 0 <= at < len(order):
            softened(order[at], at % SLOTS)
        if at < LAG:
            continue
        done = order[at - LAG]
        done_of[done] = finished(done, (at - LAG) % SLOTS)
        for n in range(1, blocks + 1):
            if done not in (n, n - 1) or n not in done_of or n - 1 not in done_of:
                continue
            token = start + (n - 1) * SPAN
            idle = (token == 0) | ((token + half_shift) % LENGTH == 0)
            kept = row >= jnp.where(idle, SPAN - 1, 0)
            for g in range(GROUP):
                before, after = done_of[n - 1][0][g], done_of[n][-1][g]
                end = jnp.where(row[-8:] == SPAN - 1, after[-8:], before[-8:])
                here = jnp.concatenate([before[:-8], end], axis=0)
                result_ref[(n - 1) * SPAN : n * SPAN, g * HD : (g + 1) * HD] = jnp.where(
                    kept, here, 0.0
                ).astype(out_ref.dtype)
            rows = pl.ds((n - 1) * SPAN, SPAN)
            copies.append(
                pltpu.make_async_copy(result_ref.at[rows], out_ref.at[rows], sems.at[n - 1])
            )
            copies[-1].start()
    for copy in copies:
        copy.wait()


def body(queries, neighbour_ids, cache_keys, cache_values, out_grad):
    holders = lax.axis_size("db")
    me = lax.axis_index("db")
    entries, entry_rows, channels = cache_keys.shape
    tokens, width = queries.shape
    spans = neighbour_ids.shape[0]
    wanted = 2 * spans
    pieces = holders // 2
    piece = entry_rows // pieces
    rows = 2
    halves = piece // rows
    chunks = entries * halves + 1
    order = exchange_order(holders)
    vmem = pl.BlockSpec(memory_space=pltpu.VMEM)
    smem = pl.BlockSpec(memory_space=pltpu.SMEM)
    hbm = pl.BlockSpec(memory_space=pltpu.HBM)
    small = pltpu.CompilerParams(vmem_limit_bytes=16 * 2**20)

    start = (me * tokens).reshape(1).astype(jnp.int32)
    packed = pl.pallas_call(
        pack_kernel,
        out_shape=jax.ShapeDtypeStruct((holders, chunks, rows, channels), jnp.bfloat16),
        in_specs=[smem] + [hbm] * 3,
        out_specs=vmem,
        scratch_shapes=[
            pltpu.SMEM((2, spans), jnp.int32),
            pltpu.SemaphoreType.DMA((2, entries)),
            pltpu.SemaphoreType.DMA,
        ],
        compiler_params=small,
    )(
        start,
        pltpu.with_memory_space_constraint(neighbour_ids.T, pltpu.HBM),
        *(
            pltpu.with_memory_space_constraint(
                x.reshape(entries, pieces, halves, rows, channels), pltpu.HBM
            )
            for x in (cache_keys, cache_values)
        ),
    )
    exchange = functools.partial(
        lax.all_to_all, axis_name="db", split_axis=0, concat_axis=0, tiled=True, axis_index_groups=[order]
    )
    spread = exchange(packed)
    ids = spread[:, chunks - 1, 0, :wanted].astype(jnp.int32) + holders * entries // 2
    places = (ids * halves + lax.div(ids, entries)).reshape(holders * wanted)
    picked = pl.pallas_call(
        functools.partial(pick_kernel, order),
        out_shape=jax.ShapeDtypeStruct((holders, halves * (wanted + 2), rows, channels), jnp.bfloat16),
        in_specs=[smem, vmem],
        out_specs=vmem,
        compiler_params=small,
    )(places, spread.reshape(holders * chunks, rows, channels))
    arrived = exchange(picked.reshape(holders, (wanted + 2) * piece, channels)).reshape(
        holders, spans + 1, 2 * piece, channels
    )
    return pl.pallas_call(
        attend_kernel,
        out_shape=jax.ShapeDtypeStruct((tokens, width), jnp.bfloat16),
        in_specs=[smem] + [vmem] * 3,
        out_specs=hbm,
        scratch_shapes=[
            pltpu.VMEM((tokens, width), jnp.bfloat16),
            pltpu.VMEM((SLOTS, GROUP * (SPAN + TAIL), 2 * entry_rows), jnp.float32),
            pltpu.VMEM((SLOTS, GROUP * (SPAN + TAIL), 2 * entry_rows), jnp.float32),
            pltpu.VMEM((SLOTS, GROUP * (SPAN + TAIL), 2 * entry_rows), jnp.bfloat16),
            pltpu.VMEM((SLOTS, GROUP * (SPAN + TAIL), HD), jnp.float32),
            pltpu.SemaphoreType.DMA((spans,)),
        ],
        compiler_params=small,
    )(start, queries, out_grad, arrived)


def solution(mesh):
    return jax.shard_map(
        body,
        mesh=mesh,
        in_specs=(
            P("db", "heads"),
            P("db", None),
            P("db", None, "heads"),
            P("db", None, "heads"),
            P("db", "heads"),
        ),
        out_specs=P("db", "heads"),
        check_vma=False,
    )
```
